32 devices in a mesh: dp: 8 (over z, core), tensor: 4 (over y, x).
Axes of the slice: x: 2, y: 2, z: 4, core: 2. Of those that a mesh axis runs over, the one named last changes fastest.
Arguments:
- tokens: bfloat16 [4096, 4096], P('dp', 'tensor'), may hold values from -6 to 6
- butterfly: bfloat16 [64, 5, 256, 256], P('tensor', None, 'dp'), may hold values from -0.15625 to 0.15625
- left_factor: bfloat16 [4096, 256], P(('tensor', 'dp')), may hold values from -0.09375 to 0.09375
- right_factor: bfloat16 [256, 16384], P('dp', 'tensor'), may hold values from -0.375 to 0.375
- cotangent: bfloat16 [4096, 16384], P('dp', 'tensor'), may hold values from -6 to 6
Outputs:
- hidden: bfloat16 [4096, 16384], P('dp', 'tensor')
- grad_tokens: bfloat16 [4096, 4096], P('dp', 'tensor')
- grad_butterfly: bfloat16 [64, 5, 256, 256], P('tensor', None, 'dp')
- grad_left: bfloat16 [4096, 256], P(('tensor', 'dp'))
- grad_right: bfloat16 [256, 16384], P('dp', 'tensor')
The draws below stay inside these ranges and needn't reach their ends.
All inputs are finite; a program needn't handle non-finite values.
Results may differ from the reference program's by a relative error of at most 0.02.
Values may be sent and summed in bfloat16 or wider, within the bound.
A program may use at most 128 MiB of HBM per device.

```python
import jax
import jax.numpy as jnp
import numpy as np
from jax import lax

D = 4096
F = 16384
BLK = 256
LOG = 4
R = 256
TOK_DEV = 512
NB = 16
HB = 64
TOKENS = 4096
N_DP = 8


def levels(own_key, extent, cuts, smallest, largest):
    gain = 1.0
    for dim, shards_of in cuts:
        draws = jax.random.uniform(jax.random.fold_in(jax.random.fold_in(own_key, 6), dim), (shards_of,), jnp.float32, smallest / len(cuts), largest / len(cuts))
        gain = gain * jnp.repeat(jnp.exp(draws), extent[dim] // shards_of).reshape((-1,) + (1,) * (len(extent) - 1 - dim))
    return gain


def noise(stream_key, shape, width, most, split=(), kind=jnp.bfloat16):
    loudness = levels(stream_key, shape, split, -0.22, 0.18) if split else 1.0
    entries = jax.random.normal(stream_key, shape, jnp.float32) * width * loudness
    return jnp.minimum(jnp.maximum(entries, -most), most).astype(kind)


def setup_inputs(seed: int = 0) -> dict:
    key_list = jax.random.split(jax.random.key(seed), 6)
    return {
        "tokens": noise(key_list[0], (TOKENS, D), 1.0, 6.0, ((0, 8), (1, 4))),
        "butterfly": noise(key_list[1], (HB, LOG + 1, BLK, BLK), ((LOG + 1) * BLK) ** -0.5, 0.15625, ((0, 4), (2, 8))),
        "left_factor": noise(key_list[2], (D, R), D ** -0.5, 0.09375, ((0, 32),)),
        "right_factor": noise(key_list[3], (R, F), R ** -0.5, 0.375, ((0, 8), (1, 4))),
        "cotangent": noise(key_list[4], (TOKENS, F), 1.0, 6.0, ((0, 8), (1, 4))),
    }


ROOT_HALF = 0.7071067811865476
INV_ROOT_TWO_PI = 0.3989422804014327


def gelu_pair(preact):
    cdf = 0.5 * (1.0 + jax.scipy.special.erf(preact * ROOT_HALF))
    return preact * cdf, cdf + preact * INV_ROOT_TWO_PI * jnp.exp(-0.5 * preact * preact)


def reference(tokens, butterfly, left_factor, right_factor, cotangent):
    group_ratio = F // D
    partner_table = [np.arange(NB)] + [np.array([index ^ (1 << level) for index in range(NB)]) for level in range(LOG)]
    weight_wide = butterfly.astype(jnp.float32).reshape(NB, group_ratio, LOG + 1, BLK, BLK)
    token_groups = tokens.reshape(N_DP, TOK_DEV, D)
    cot_groups = cotangent.reshape(N_DP, TOK_DEV, F)
    highest = lax.Precision.HIGHEST

    def one_group(totals, inputs_pair):
        token_group, cot_group = inputs_pair
        blocks = token_group.astype(jnp.float32).reshape(TOK_DEV, NB, BLK)
        preact = jnp.zeros((TOK_DEV, NB, group_ratio, BLK), jnp.float32)
        for factor in range(LOG + 1):
            partner = blocks[:, partner_table[factor]]
            preact = preact + jnp.einsum("tgi,grio->tgro", partner, weight_wide[:, :, factor], precision=highest)
        low_rank = jnp.dot(token_group, left_factor, preferred_element_type=jnp.float32).astype(jnp.bfloat16)
        preact = preact.reshape(TOK_DEV, F) + jnp.dot(low_rank, right_factor, preferred_element_type=jnp.float32)
        activation, slopes = gelu_pair(preact)
        grad_pre = (cot_group.astype(jnp.float32) * slopes).astype(jnp.bfloat16)
        grad_wide = grad_pre.astype(jnp.float32).reshape(TOK_DEV, NB, group_ratio, BLK)
        grads = []
        grad_blocks = jnp.zeros((TOK_DEV, NB, BLK), jnp.float32)
        for factor in range(LOG + 1):
            partner = blocks[:, partner_table[factor]]
            grads.append(jnp.einsum("tgi,tgro->grio", partner, grad_wide, precision=highest))
            contrib = jnp.einsum("tgro,grio->tgi", grad_wide, weight_wide[:, :, factor], precision=highest)
            grad_blocks = grad_blocks + contrib[:, partner_table[factor]]
        grad_weight = jnp.stack(grads, axis=2).reshape(HB, LOG + 1, BLK, BLK)
        grad_low = jnp.dot(grad_pre, right_factor.T, preferred_element_type=jnp.float32).astype(jnp.bfloat16)
        grad_input = grad_blocks.reshape(TOK_DEV, D) + jnp.dot(grad_low, left_factor.T, preferred_element_type=jnp.float32)
        grad_first = jnp.dot(token_group.T, grad_low, preferred_element_type=jnp.float32)
        grad_second = jnp.dot(low_rank.T, grad_pre, preferred_element_type=jnp.float32)
        rounded = lax.optimization_barrier((grad_weight.astype(jnp.bfloat16), grad_first.astype(jnp.bfloat16), grad_second.astype(jnp.bfloat16)))
        totals = (totals[0] + rounded[0].astype(jnp.float32), totals[1] + rounded[1].astype(jnp.float32), totals[2] + rounded[2].astype(jnp.float32))
        return totals, (activation.astype(jnp.bfloat16), grad_input.astype(jnp.bfloat16))

    start = (jnp.zeros((HB, LOG + 1, BLK, BLK), jnp.float32), jnp.zeros((D, R), jnp.float32), jnp.zeros((R, F), jnp.float32))
    totals, outputs = lax.scan(one_group, start, (token_groups, cot_groups))
    hidden = outputs[0].reshape(TOKENS, F)
    grad_tokens = outputs[1].reshape(TOKENS, D)
    return (hidden, grad_tokens, totals[0].astype(jnp.bfloat16), totals[1].astype(jnp.bfloat16), totals[2].astype(jnp.bfloat16))
```

```python
import functools

import jax
import jax.numpy as jnp
from jax import lax
from jax.experimental import pallas as pl
from jax.experimental.pallas import tpu as pltpu
from jax.sharding import PartitionSpec as P

BLK = 256
LOG = 4


ROOT_HALF = 0.7071067811865476
INV_ROOT_TWO_PI = 0.3989422804014327
BF16 = jnp.bfloat16
F32 = jnp.float32


def swapped(block, axis, mask):
    count = lax.axis_size(axis)
    return lax.ppermute(block, axis, [(i, i ^ mask) for i in range(count)])


def summed_over(part, axis):
    count = lax.axis_size(axis)
    total = part.astype(F32)
    for mask in range(1, count):
        total = total + swapped(part, axis, mask).astype(F32)
    return total.astype(BF16)


def gelu_pair(preact):
    cdf = 0.5 * (1.0 + lax.erf(preact * ROOT_HALF))
    return (preact * cdf, cdf + preact * INV_ROOT_TWO_PI * jnp.exp(-0.5 * preact * preact))


def nt_dot(a, b):
    return lax.dot_general(a, b, (((1,), (1,)), ((), ())), preferred_element_type=F32)


def chunk_kernel(factors, local, aliased, *refs):
    pieces = refs[:factors]
    cot_ref, w_ref = refs[factors:factors + 2]
    rest = refs[factors + 2 + (1 if aliased else 0):]
    hidden_ref, dw_ref, loc_ref = rest[:3]
    far_refs = rest[3:3 + factors - 1 - local]
    low_ref = rest[3 + factors - 1 - local]
    x, xt, acc = rest[-3:]
    step = pl.program_id(0)

    @pl.when(step == 0)
    def _():
        for k in range(factors):
            piece = pieces[k][...]
            x[:, k * BLK:(k + 1) * BLK] = piece
            xt[k * BLK:(k + 1) * BLK, :] = piece.T

    w = w_ref[0]
    preact = jnp.dot(x[...], w, preferred_element_type=F32)
    act, slope = gelu_pair(preact)
    hidden_ref[...] = act.astype(BF16)
    grad = (cot_ref[...].astype(F32) * slope).astype(BF16)
    dw_ref[0] = jnp.dot(xt[...], grad, preferred_element_type=F32).astype(BF16)
    back = nt_dot(grad, w)

    @pl.when(step == 0)
    def _():
        acc[...] = back

    @pl.when(step > 0)
    def _():
        acc[...] += back

    @pl.when(step == pl.num_programs(0) - 1)
    def _():
        loc_ref[...] = acc[:, :local * BLK]
        for i, far in enumerate(far_refs):
            far[...] = acc[:, (local + i) * BLK:(local + i + 1) * BLK].astype(BF16)
        low_ref[...] = acc[:, (factors - 1) * BLK:]


def run_chunk(q, ratio, local, piece_arrays, piece_cols, cot, w, hidden_prev):
    rows, wide = cot.shape
    factors = len(piece_arrays)
    depth = factors * BLK
    n_far = factors - 1 - local
    column = lambda col: pl.BlockSpec((rows, BLK), lambda h: (0, col))
    in_specs = [column(col) for col in piece_cols]
    in_specs += [
        pl.BlockSpec((rows, BLK), lambda h: (0, q * ratio + h)),
        pl.BlockSpec((1, depth, BLK), lambda h: (h, 0, 0)),
    ]
    args = list(piece_arrays) + [cot, w]
    aliases = {}
    if hidden_prev is not None:
        aliases = {len(args): 0}
        args.append(hidden_prev)
        in_specs.append(pl.BlockSpec(memory_space=pl.ANY))
    whole = lambda cols: pl.BlockSpec((rows, cols), lambda h: (0, 0))
    out_specs = [
        pl.BlockSpec((rows, BLK), lambda h: (0, q * ratio + h)),
        pl.BlockSpec((1, depth, BLK), lambda h: (h, 0, 0)),
        whole(local * BLK),
    ] + [whole(BLK)] * (n_far + 1)
    out_shape = [
        jax.ShapeDtypeStruct((rows, wide), BF16),
        jax.ShapeDtypeStruct((ratio, depth, BLK), BF16),
        jax.ShapeDtypeStruct((rows, local * BLK), F32),
    ] + [jax.ShapeDtypeStruct((rows, BLK), BF16)] * n_far + [jax.ShapeDtypeStruct((rows, BLK), F32)]
    return pl.pallas_call(
        functools.partial(chunk_kernel, factors, local, hidden_prev is not None),
        grid=(ratio,),
        in_specs=in_specs,
        out_specs=out_specs,
        out_shape=out_shape,
        scratch_shapes=[
            pltpu.VMEM((rows, depth), BF16),
            pltpu.VMEM((depth, rows), BF16),
            pltpu.VMEM((rows, depth), F32),
        ],
        input_output_aliases=aliases,
        cost_estimate=pl.CostEstimate(
            flops=6 * rows * depth * BLK * ratio,
            bytes_accessed=2 * (2 * ratio * depth * BLK + 2 * rows * ratio * BLK + 5 * rows * depth // 2),
            transcendentals=2 * rows * ratio * BLK,
        ),
        compiler_params=pltpu.CompilerParams(
            dimension_semantics=("arbitrary",), vmem_limit_bytes=40 * 1024 * 1024
        ),
    )(*args)


def final_kernel(blocks, local_masks, n_far, *refs):
    locs = refs[:blocks]
    fars = refs[blocks:blocks + n_far * blocks]
    grad_low, left, out = refs[blocks + n_far * blocks:]
    for j in range(blocks):
        total = nt_dot(grad_low[...], left[j * BLK:(j + 1) * BLK, :])
        for k, mask in enumerate(local_masks):
            total = total + locs[j ^ mask][:, k * BLK:(k + 1) * BLK]
        for i in range(n_far):
            total = total + fars[i * blocks + j][...].astype(F32)
        out[:, j * BLK:(j + 1) * BLK] = total.astype(BF16)


def per_device(tokens, butterfly, left_factor, right_factor, cotangent):
    rows = tokens.shape[0]
    blocks = tokens.shape[1] // BLK
    hidden_blocks = right_factor.shape[1] // BLK
    share = right_factor.shape[0]
    ratio = hidden_blocks // blocks
    local_masks = [0] + [1 << b for b in range(LOG) if 1 << b < blocks]
    far_masks = [(1 << b) // blocks for b in range(LOG) if 1 << b >= blocks]
    n_far = len(far_masks)
    factors = LOG + 2

    right_blocks = right_factor.reshape(share, hidden_blocks, BLK).transpose(1, 0, 2)
    weights = []
    for q in range(blocks):
        part = slice(q * ratio, (q + 1) * ratio)
        local_w = jnp.concatenate([butterfly[part], right_blocks[part][:, None]], axis=1)
        full = lax.all_gather(local_w, "dp", axis=2, tiled=True)
        weights.append(full.reshape(ratio, factors * BLK, BLK))

    left_full = lax.all_gather(left_factor, "dp", axis=0, tiled=True)
    far_tokens = [swapped(tokens, "tensor", mask) for mask in far_masks]
    low_part = jnp.dot(tokens, left_full, preferred_element_type=F32).astype(BF16)
    low = summed_over(low_part, "tensor")

    hidden = None
    locs, fars, low_back, grads = [], [[] for _ in far_masks], None, []
    for q in range(blocks):
        arrays = [tokens] * len(local_masks) + far_tokens + [low]
        columns = [q ^ mask for mask in local_masks] + [q] * n_far + [0]
        hidden, dw, loc, *more = run_chunk(
            q, ratio, len(local_masks), arrays, columns, cotangent, weights[q], hidden
        )
        grads.append(
            lax.psum_scatter(
                dw.reshape(ratio, factors, BLK, BLK), "dp", scatter_dimension=2, tiled=True
            )
        )
        locs.append(loc)
        for i, mask in enumerate(far_masks):
            fars[i].append(swapped(more[i], "tensor", mask))
        low_back = more[-1] if low_back is None else low_back + more[-1]

    grad_low = summed_over(low_back.astype(BF16), "tensor")
    grad_first = jnp.einsum("td,tr->dr", tokens, grad_low, preferred_element_type=F32)
    sum_first = lax.psum_scatter(grad_first.astype(BF16), "dp", scatter_dimension=0, tiled=True)
    grad_tokens = pl.pallas_call(
        functools.partial(final_kernel, blocks, local_masks, n_far),
        out_shape=jax.ShapeDtypeStruct(tokens.shape, BF16),
        in_specs=[pl.BlockSpec(memory_space=pltpu.VMEM)] * (blocks + n_far * blocks + 2),
        out_specs=pl.BlockSpec(memory_space=pltpu.VMEM),
        cost_estimate=pl.CostEstimate(
            flops=2 * rows * blocks * BLK * BLK,
            bytes_accessed=rows * blocks * BLK * (4 * len(local_masks) + 2 * n_far + 2),
            transcendentals=0,
        ),
        compiler_params=pltpu.CompilerParams(vmem_limit_bytes=40 * 1024 * 1024),
    )(*locs, *[f for level in fars for f in level], grad_low, left_full)

    grad_all = jnp.concatenate(grads, axis=0)
    sum_weight = grad_all[:, :LOG + 1]
    sum_second = grad_all[:, LOG + 1].transpose(1, 0, 2).reshape(share, hidden_blocks * BLK)
    return (hidden, grad_tokens, sum_weight, sum_first, sum_second)


def solution(mesh):
    placed = (
        P("dp", "tensor"),
        P("tensor", None, "dp", None),
        P(("tensor", "dp"), None),
        P("dp", "tensor"),
        P("dp", "tensor"),
    )
    return jax.shard_map(
        per_device,
        mesh=mesh,
        in_specs=placed,
        out_specs=(
            P("dp", "tensor"),
            P("dp", "tensor"),
            P("tensor", None, "dp", None),
            P(("tensor", "dp"), None),
            P("dp", "tensor"),
        ),
        check_vma=False,
    )
```

```python
import functools

import jax
import jax.numpy as jnp
from jax import lax
from jax.experimental import pallas as pl
from jax.experimental.pallas import tpu as pltpu
from jax.sharding import PartitionSpec as P

BLK = 256
LOG = 4


ROOT_HALF = 0.7071067811865476
INV_ROOT_TWO_PI = 0.3989422804014327
BF16 = jnp.bfloat16
F32 = jnp.float32
GATHER_LINES = (0, 1, 3)
SCATTER_LINES = (2, 3)


def swapped(block, axis, mask):
    count = lax.axis_size(axis)
    return lax.ppermute(block, axis, [(i, i ^ mask) for i in range(count)])


def summed_over(part, axis):
    count = lax.axis_size(axis)
    total = part.astype(F32)
    for mask in range(1, count):
        total = total + swapped(part, axis, mask).astype(F32)
    return total.astype(BF16)


def gelu_pair(preact):
    cdf = 0.5 * (1.0 + lax.erf(preact * ROOT_HALF))
    return (preact * cdf, cdf + preact * INV_ROOT_TWO_PI * jnp.exp(-0.5 * preact * preact))


def nt_dot(a, b):
    return lax.dot_general(a, b, (((1,), (1,)), ((), ())), preferred_element_type=F32)


def core_swap(x):
    return swapped(x, "dp", 1)


def moved(x, shift, sources):
    pairs = [(2 * p + c, 2 * (p + shift) + c) for p in sources for c in range(2)]
    return lax.ppermute(x, "dp", pairs)


def line_gather(x):
    chips = lax.axis_size("dp") // 2
    chip = lax.axis_index("dp") // 2
    from_left, from_right = [x], [x]
    for step in range(1, chips):
        from_left.append(moved(from_left[-1], 1, range(step - 1, chips - 1)))
        from_right.append(moved(from_right[-1], -1, range(1, chips - step + 1)))
    slots = [x] + [
        jnp.where(chip >= j, from_left[j], from_right[chips - j]) for j in range(1, chips)
    ]
    own = jnp.stack(slots)
    return own, core_swap(own)


def line_scatter(mine, theirs):
    chips = lax.axis_size("dp") // 2
    chip = lax.axis_index("dp") // 2
    pair = (mine.astype(F32) + core_swap(theirs).astype(F32)).astype(BF16)
    pick = lambda index: lax.dynamic_index_in_dim(
        pair, jnp.clip(index, 0, chips - 1), 0, keepdims=False
    ).astype(F32)
    right = left = None
    for step in range(1, chips):
        going_right, going_left = pick(chip + chips - step), pick(chip - chips + step)
        if right is not None:
            going_right = going_right + right.astype(F32)
            going_left = going_left + left.astype(F32)
        right = moved(going_right.astype(BF16), 1, range(0, step))
        left = moved(going_left.astype(BF16), -1, range(chips - step, chips))
    return (pick(chip) + right.astype(F32) + left.astype(F32)).astype(BF16)


def chunk_kernel(factors, local, aliased, line_in, line_out, place_ref, *refs):
    pieces = refs[:factors]
    cot_ref = refs[factors]
    w_refs = refs[factors + 1:factors + 2 + line_in]
    rest = refs[factors + 2 + line_in + aliased:]
    hidden_ref = rest[0]
    dw_refs = rest[1:2 + line_out]
    loc_ref = rest[2 + line_out]
    far_refs = rest[3 + line_out:3 + line_out + factors - 1 - local]
    low_ref = rest[2 + line_out + factors - local]
    x, xt, acc, wide = rest[-4:]
    step = pl.program_id(0)
    chip, core = place_ref[0], place_ref[1]
    chips, share = wide.shape[1], wide.shape[3]
    depth = factors * BLK

    @pl.when(step == 0)
    def _():
        for k in range(factors):
            piece = pieces[k][...]
            x[:, k * BLK:(k + 1) * BLK] = piece
            xt[k * BLK:(k + 1) * BLK, :] = piece.T

    if line_in:
        for s in range(chips):
            slot = lax.rem(chip - s + chips, chips)
            for k in range(factors):
                wide[k, s, core] = w_refs[0][slot, 0, k]
                wide[k, s, 1 - core] = w_refs[1][slot, 0, k]
        w = wide[...].reshape(depth, BLK)
    else:
        w = w_refs[0][0]
    preact = jnp.dot(x[...], w, preferred_element_type=F32)
    act, slope = gelu_pair(preact)
    hidden_ref[...] = act.astype(BF16)
    grad = (cot_ref[...].astype(F32) * slope).astype(BF16)
    back = nt_dot(grad, w)

    @pl.when(step == 0)
    def _():
        acc[...] = back

    @pl.when(step > 0)
    def _():
        acc[...] += back

    dw = jnp.dot(xt[...], grad, preferred_element_type=F32).astype(BF16)
    if line_out:
        wide[...] = dw.reshape(wide.shape)
        for s in range(chips):
            for k in range(factors):
                dw_refs[0][s, 0, k] = wide[k, s, core]
                dw_refs[1][s, 0, k] = wide[k, s, 1 - core]
    else:
        dw_refs[0][0] = dw

    @pl.when(step == pl.num_programs(0) - 1)
    def _():
        loc_ref[...] = acc[:, :local * BLK]
        for i, far in enumerate(far_refs):
            far[...] = acc[:, (local + i) * BLK:(local + i + 1) * BLK].astype(BF16)
        low_ref[...] = acc[:, (factors - 1) * BLK:]


def run_chunk(q, ratio, local, piece_arrays, piece_cols, cot, weights, hidden_prev, chips, line_out):
    rows, wide = cot.shape
    factors = len(piece_arrays)
    depth = factors * BLK
    share = BLK // (2 * chips)
    n_far = factors - 1 - local
    line_in = len(weights) == 2
    place = jnp.stack([lax.axis_index("dp") // 2, lax.axis_index("dp") % 2])
    column = lambda col: pl.BlockSpec((rows, BLK), lambda h: (0, col))
    plain = pl.BlockSpec((1, depth, BLK), lambda h: (h, 0, 0))
    lined = pl.BlockSpec((chips, 1, factors, share, BLK), lambda h: (0, h, 0, 0, 0))
    in_specs = [pl.BlockSpec(memory_space=pltpu.SMEM)]
    in_specs += [column(col) for col in piece_cols]
    in_specs += [pl.BlockSpec((rows, BLK), lambda h: (0, q * ratio + h))]
    in_specs += [lined, lined] if line_in else [plain]
    args = [place] + list(piece_arrays) + [cot] + list(weights)
    aliases = {}
    if hidden_prev is not None:
        aliases = {len(args): 0}
        args.append(hidden_prev)
        in_specs.append(pl.BlockSpec(memory_space=pl.ANY))
    whole = lambda cols: pl.BlockSpec((rows, cols), lambda h: (0, 0))
    out_specs = [pl.BlockSpec((rows, BLK), lambda h: (0, q * ratio + h))]
    out_specs += [lined, lined] if line_out else [plain]
    out_specs += [whole(local * BLK)] + [whole(BLK)] * (n_far + 1)
    lined_shape = jax.ShapeDtypeStruct((chips, ratio, factors, share, BLK), BF16)
    out_shape = [jax.ShapeDtypeStruct((rows, wide), BF16)]
    out_shape += [lined_shape] * 2 if line_out else [jax.ShapeDtypeStruct((ratio, depth, BLK), BF16)]
    out_shape += [jax.ShapeDtypeStruct((rows, local * BLK), F32)]
    out_shape += [jax.ShapeDtypeStruct((rows, BLK), BF16)] * n_far
    out_shape += [jax.ShapeDtypeStruct((rows, BLK), F32)]
    outs = pl.pallas_call(
        functools.partial(chunk_kernel, factors, local, int(hidden_prev is not None), int(line_in), int(line_out)),
        grid=(ratio,),
        in_specs=in_specs,
        out_specs=out_specs,
        out_shape=out_shape,
        scratch_shapes=[
            pltpu.VMEM((rows, depth), BF16),
            pltpu.VMEM((depth, rows), BF16),
            pltpu.VMEM((rows, depth), F32),
            pltpu.VMEM((factors, chips, 2, share, BLK), BF16),
        ],
        input_output_aliases=aliases,
        cost_estimate=pl.CostEstimate(
            flops=6 * rows * depth * BLK * ratio,
            bytes_accessed=2 * (2 * ratio * depth * BLK + 2 * rows * ratio * BLK + 5 * rows * depth // 2),
            transcendentals=2 * rows * ratio * BLK,
        ),
        compiler_params=pltpu.CompilerParams(
            dimension_semantics=("arbitrary",), vmem_limit_bytes=40 * 1024 * 1024
        ),
    )(*args)
    dw = outs[1:2 + int(line_out)]
    return outs[0], dw, outs[2 + int(line_out)], outs[3 + int(line_out):]


def final_kernel(blocks, local_masks, n_far, *refs):
    locs = refs[:blocks]
    fars = refs[blocks:blocks + n_far * blocks]
    grad_low, left, out = refs[blocks + n_far * blocks:]
    for j in range(blocks):
        total = nt_dot(grad_low[...], left[j * BLK:(j + 1) * BLK, :])
        for k, mask in enumerate(local_masks):
            total = total + locs[j ^ mask][:, k * BLK:(k + 1) * BLK]
        for i in range(n_far):
            total = total + fars[i * blocks + j][...].astype(F32)
        out[:, j * BLK:(j + 1) * BLK] = total.astype(BF16)


def per_device(tokens, butterfly, left_factor, right_factor, cotangent):
    rows = tokens.shape[0]
    blocks = tokens.shape[1] // BLK
    hidden_blocks = right_factor.shape[1] // BLK
    share = right_factor.shape[0]
    ratio = hidden_blocks // blocks
    local_masks = [0] + [1 << b for b in range(LOG) if 1 << b < blocks]
    far_masks = [(1 << b) // blocks for b in range(LOG) if 1 << b >= blocks]
    n_far = len(far_masks)
    factors = LOG + 2
    chips = lax.axis_size("dp") // 2
    short = chips <= 4 and blocks >= 4 and share % 16 == 0
    gather_lines = GATHER_LINES if short else ()
    scatter_lines = SCATTER_LINES if short else ()

    right_blocks = right_factor.reshape(share, hidden_blocks, BLK).transpose(1, 0, 2)
    weights = []
    for q in range(blocks):
        part = slice(q * ratio, (q + 1) * ratio)
        local_w = jnp.concatenate([butterfly[part], right_blocks[part][:, None]], axis=1)
        if q in gather_lines:
            weights.append(line_gather(local_w))
        else:
            full = lax.all_gather(local_w, "dp", axis=2, tiled=True)
            weights.append((full.reshape(ratio, factors * BLK, BLK),))

    left_full = lax.all_gather(left_factor, "dp", axis=0, tiled=True)
    far_tokens = [swapped(tokens, "tensor", mask) for mask in far_masks]
    low_part = jnp.dot(tokens, left_full, preferred_element_type=F32).astype(BF16)
    low = summed_over(low_part, "tensor")

    hidden = None
    locs, fars, low_back, grads = [], [[] for _ in far_masks], None, []
    for q in range(blocks):
        arrays = [tokens] * len(local_masks) + far_tokens + [low]
        columns = [q ^ mask for mask in local_masks] + [q] * n_far + [0]
        hidden, dw, loc, more = run_chunk(
            q, ratio, len(local_masks), arrays, columns, cotangent, weights[q], hidden,
            chips, q in scatter_lines,
        )
        if q in scatter_lines:
            grads.append(line_scatter(*dw))
        else:
            grads.append(
                lax.psum_scatter(
                    dw[0].reshape(ratio, factors, BLK, BLK), "dp", scatter_dimension=2, tiled=True
                )
            )
        locs.append(loc)
        for i, mask in enumerate(far_masks):
            fars[i].append(swapped(more[i], "tensor", mask))
        low_back = more[-1] if low_back is None else low_back + more[-1]

    grad_low = summed_over(low_back.astype(BF16), "tensor")
    grad_first = jnp.einsum("td,tr->dr", tokens, grad_low, preferred_element_type=F32)
    grad_first = grad_first.astype(BF16)
    if short:
        by_owner = grad_first.reshape(chips, 2, -1, BLK)
        core = lax.axis_index("dp") % 2
        mine = lax.dynamic_index_in_dim(by_owner, core, 1, keepdims=False)
        theirs = lax.dynamic_index_in_dim(by_owner, 1 - core, 1, keepdims=False)
        sum_first = line_scatter(mine, theirs)
    else:
        sum_first = lax.psum_scatter(grad_first, "dp", scatter_dimension=0, tiled=True)
    grad_tokens = pl.pallas_call(
        functools.partial(final_kernel, blocks, local_masks, n_far),
        out_shape=jax.ShapeDtypeStruct(tokens.shape, BF16),
        in_specs=[pl.BlockSpec(memory_space=pltpu.VMEM)] * (blocks + n_far * blocks + 2),
        out_specs=pl.BlockSpec(memory_space=pltpu.VMEM),
        cost_estimate=pl.CostEstimate(
            flops=2 * rows * blocks * BLK * BLK,
            bytes_accessed=rows * blocks * BLK * (4 * len(local_masks) + 2 * n_far + 2),
            transcendentals=0,
        ),
        compiler_params=pltpu.CompilerParams(vmem_limit_bytes=40 * 1024 * 1024),
    )(*locs, *[f for level in fars for f in level], grad_low, left_full)

    grad_all = jnp.concatenate(grads, axis=0)
    sum_weight = grad_all[:, :LOG + 1]
    sum_second = grad_all[:, LOG + 1].transpose(1, 0, 2).reshape(share, hidden_blocks * BLK)
    return (hidden, grad_tokens, sum_weight, sum_first, sum_second)


def solution(mesh):
    placed = (
        P("dp", "tensor"),
        P("tensor", None, "dp", None),
        P(("tensor", "dp"), None),
        P("dp", "tensor"),
        P("dp", "tensor"),
    )
    return jax.shard_map(
        per_device,
        mesh=mesh,
        in_specs=placed,
        out_specs=(
            P("dp", "tensor"),
            P("dp", "tensor"),
            P("tensor", None, "dp", None),
            P(("tensor", "dp"), None),
            P("dp", "tensor"),
        ),
        check_vma=False,
    )
```

```python
import functools

import jax
import jax.numpy as jnp
from jax import lax
from jax.experimental import pallas as pl
from jax.experimental.pallas import tpu as pltpu
from jax.sharding import PartitionSpec as P

BLK = 256
LOG = 4


ROOT_HALF = 0.7071067811865476
INV_ROOT_TWO_PI = 0.3989422804014327
BF16 = jnp.bfloat16
F32 = jnp.float32


def swapped(block, axis, mask):
    count = lax.axis_size(axis)
    return lax.ppermute(block, axis, [(i, i ^ mask) for i in range(count)])


def summed_over(part, axis):
    count = lax.axis_size(axis)
    total = part.astype(F32)
    for mask in range(1, count):
        total = total + swapped(part, axis, mask).astype(F32)
    return total.astype(BF16)


def gelu_pair(preact):
    cdf = 0.5 * (1.0 + lax.erf(preact * ROOT_HALF))
    return (preact * cdf, cdf + preact * INV_ROOT_TWO_PI * jnp.exp(-0.5 * preact * preact))


def nt_dot(a, b):
    return lax.dot_general(a, b, (((1,), (1,)), ((), ())), preferred_element_type=F32)


def core_swap(x):
    return swapped(x, "dp", 1)


def moved(x, shift, sources):
    pairs = [(2 * p + c, 2 * (p + shift) + c) for p in sources for c in range(2)]
    return lax.ppermute(x, "dp", pairs)


def line_scatter(mine, theirs):
    chips = lax.axis_size("dp") // 2
    chip = lax.axis_index("dp") // 2
    pair = (mine.astype(F32) + core_swap(theirs).astype(F32)).astype(BF16)
    pick = lambda index: lax.dynamic_index_in_dim(
        pair, jnp.clip(index, 0, chips - 1), 0, keepdims=False
    ).astype(F32)
    right = left = None
    for step in range(1, chips):
        going_right, going_left = pick(chip + chips - step), pick(chip - chips + step)
        if right is not None:
            going_right = going_right + right.astype(F32)
            going_left = going_left + left.astype(F32)
        right = moved(going_right.astype(BF16), 1, range(0, step))
        left = moved(going_left.astype(BF16), -1, range(chips - step, chips))
    return (pick(chip) + right.astype(F32) + left.astype(F32)).astype(BF16)


def chunk_kernel(factors, local, aliased, *refs):
    pieces = refs[:factors]
    cot_ref, w_ref = refs[factors:factors + 2]
    rest = refs[factors + 2 + aliased:]
    hidden_ref, dw_ref, loc_ref = rest[:3]
    far_refs = rest[3:3 + factors - 1 - local]
    low_ref = rest[3 + factors - 1 - local]
    x, xt, acc = rest[-3:]
    step = pl.program_id(0)

    @pl.when(step == 0)
    def _():
        for k in range(factors):
            piece = pieces[k][...]
            x[:, k * BLK:(k + 1) * BLK] = piece
            xt[k * BLK:(k + 1) * BLK, :] = piece.T

    w = w_ref[0]
    preact = jnp.dot(x[...], w, preferred_element_type=F32)
    act, slope = gelu_pair(preact)
    hidden_ref[...] = act.astype(BF16)
    grad = (cot_ref[...].astype(F32) * slope).astype(BF16)
    dw_ref[0] = jnp.dot(xt[...], grad, preferred_element_type=F32).astype(BF16)
    back = nt_dot(grad, w)

    @pl.when(step == 0)
    def _():
        acc[...] = back

    @pl.when(step > 0)
    def _():
        acc[...] += back

    @pl.when(step == pl.num_programs(0) - 1)
    def _():
        loc_ref[...] = acc[:, :local * BLK]
        for i, far in enumerate(far_refs):
            far[...] = acc[:, (local + i) * BLK:(local + i + 1) * BLK].astype(BF16)
        low_ref[...] = acc[:, (factors - 1) * BLK:]


def run_chunk(q, at, ratio, local, piece_arrays, piece_cols, cot, w, hidden_prev, dw_prev):
    rows, wide = cot.shape
    factors = len(piece_arrays)
    depth = factors * BLK
    n_far = factors - 1 - local
    column = lambda col: pl.BlockSpec((rows, BLK), lambda h: (0, col))
    in_specs = [column(col) for col in piece_cols]
    in_specs += [
        pl.BlockSpec((rows, BLK), lambda h: (0, q * ratio + h)),
        pl.BlockSpec((1, depth, BLK), lambda h: (at * ratio + h, 0, 0)),
    ]
    args = list(piece_arrays) + [cot, w]
    aliases = {}
    for output, previous in enumerate((hidden_prev, dw_prev)):
        if previous is not None:
            aliases[len(args)] = output
            args.append(previous)
            in_specs.append(pl.BlockSpec(memory_space=pl.ANY))
    whole = lambda cols: pl.BlockSpec((rows, cols), lambda h: (0, 0))
    out_specs = [
        pl.BlockSpec((rows, BLK), lambda h: (0, q * ratio + h)),
        pl.BlockSpec((1, depth, BLK), lambda h: (at * ratio + h, 0, 0)),
        whole(local * BLK),
    ] + [whole(BLK)] * (n_far + 1)
    out_shape = [
        jax.ShapeDtypeStruct((rows, wide), BF16),
        jax.ShapeDtypeStruct(w.shape, BF16),
        jax.ShapeDtypeStruct((rows, local * BLK), F32),
    ] + [jax.ShapeDtypeStruct((rows, BLK), BF16)] * n_far + [jax.ShapeDtypeStruct((rows, BLK), F32)]
    return pl.pallas_call(
        functools.partial(chunk_kernel, factors, local, len(aliases)),
        grid=(ratio,),
        in_specs=in_specs,
        out_specs=out_specs,
        out_shape=out_shape,
        scratch_shapes=[
            pltpu.VMEM((rows, depth), BF16),
            pltpu.VMEM((depth, rows), BF16),
            pltpu.VMEM((rows, depth), F32),
        ],
        input_output_aliases=aliases,
        cost_estimate=pl.CostEstimate(
            flops=6 * rows * depth * BLK * ratio,
            bytes_accessed=2 * (2 * ratio * depth * BLK + 2 * rows * ratio * BLK + 5 * rows * depth // 2),
            transcendentals=2 * rows * ratio * BLK,
        ),
        compiler_params=pltpu.CompilerParams(
            dimension_semantics=("arbitrary",), vmem_limit_bytes=40 * 1024 * 1024
        ),
    )(*args)


def final_kernel(blocks, local_masks, n_far, *refs):
    locs = refs[:blocks]
    fars = refs[blocks:blocks + n_far * blocks]
    grad_low, left, out = refs[blocks + n_far * blocks:]
    for j in range(blocks):
        total = nt_dot(grad_low[...], left[j * BLK:(j + 1) * BLK, :])
        for k, mask in enumerate(local_masks):
            total = total + locs[j ^ mask][:, k * BLK:(k + 1) * BLK]
        for i in range(n_far):
            total = total + fars[i * blocks + j][...].astype(F32)
        out[:, j * BLK:(j + 1) * BLK] = total.astype(BF16)


def per_device(tokens, butterfly, left_factor, right_factor, cotangent):
    rows = tokens.shape[0]
    blocks = tokens.shape[1] // BLK
    hidden_blocks = right_factor.shape[1] // BLK
    share = right_factor.shape[0]
    ratio = hidden_blocks // blocks
    local_masks = [0] + [1 << b for b in range(LOG) if 1 << b < blocks]
    far_masks = [(1 << b) // blocks for b in range(LOG) if 1 << b >= blocks]
    n_far = len(far_masks)
    factors = LOG + 2
    chips = lax.axis_size("dp") // 2

    right_blocks = right_factor.reshape(share, hidden_blocks, BLK).transpose(1, 0, 2)
    weights = []
    span = max(1, blocks // 2)
    for first in range(0, blocks, span):
        part = slice(first * ratio, (first + span) * ratio)
        local_w = jnp.concatenate([butterfly[part], right_blocks[part][:, None]], axis=1)
        full = lax.all_gather(local_w, "dp", axis=2, tiled=True)
        weights.append(full.reshape(span * ratio, factors * BLK, BLK))

    left_full = lax.all_gather(left_factor, "dp", axis=0, tiled=True)
    far_tokens = [swapped(tokens, "tensor", mask) for mask in far_masks]
    low_part = jnp.dot(tokens, left_full, preferred_element_type=F32).astype(BF16)
    low = summed_over(low_part, "tensor")

    hidden = dw = None
    locs, fars, low_back, grads = [], [[] for _ in far_masks], None, []
    for q in range(blocks):
        at = q % span
        arrays = [tokens] * len(local_masks) + far_tokens + [low]
        columns = [q ^ mask for mask in local_masks] + [q] * n_far + [0]
        hidden, dw, loc, *more = run_chunk(
            q, at, ratio, len(local_masks), arrays, columns, cotangent, weights[q // span],
            hidden, dw if at else None,
        )
        if at == span - 1:
            blocks_dw = dw.reshape(span * ratio, factors, BLK, BLK)
            grads.append(lax.psum_scatter(blocks_dw, "dp", scatter_dimension=2, tiled=True))
        locs.append(loc)
        for i, mask in enumerate(far_masks):
            fars[i].append(swapped(more[i], "tensor", mask))
        low_back = more[-1] if low_back is None else low_back + more[-1]

    grad_low = summed_over(low_back.astype(BF16), "tensor")
    grad_first = jnp.einsum("td,tr->dr", tokens, grad_low, preferred_element_type=F32)
    grad_first = grad_first.astype(BF16)
    if chips <= 4:
        by_owner = grad_first.reshape(chips, 2, -1, BLK)
        core = lax.axis_index("dp") % 2
        mine = lax.dynamic_index_in_dim(by_owner, core, 1, keepdims=False)
        theirs = lax.dynamic_index_in_dim(by_owner, 1 - core, 1, keepdims=False)
        sum_first = line_scatter(mine, theirs)
    else:
        sum_first = lax.psum_scatter(grad_first, "dp", scatter_dimension=0, tiled=True)
    grad_tokens = pl.pallas_call(
        functools.partial(final_kernel, blocks, local_masks, n_far),
        out_shape=jax.ShapeDtypeStruct(tokens.shape, BF16),
        in_specs=[pl.BlockSpec(memory_space=pltpu.VMEM)] * (blocks + n_far * blocks + 2),
        out_specs=pl.BlockSpec(memory_space=pltpu.VMEM),
        cost_estimate=pl.CostEstimate(
            flops=2 * rows * blocks * BLK * BLK,
            bytes_accessed=rows * blocks * BLK * (4 * len(local_masks) + 2 * n_far + 2),
            transcendentals=0,
        ),
        compiler_params=pltpu.CompilerParams(vmem_limit_bytes=40 * 1024 * 1024),
    )(*locs, *[f for level in fars for f in level], grad_low, left_full)

    grad_all = jnp.concatenate(grads, axis=0)
    sum_weight = grad_all[:, :LOG + 1]
    sum_second = grad_all[:, LOG + 1].transpose(1, 0, 2).reshape(share, hidden_blocks * BLK)
    return (hidden, grad_tokens, sum_weight, sum_first, sum_second)


def solution(mesh):
    placed = (
        P("dp", "tensor"),
        P("tensor", None, "dp", None),
        P(("tensor", "dp"), None),
        P("dp", "tensor"),
        P("dp", "tensor"),
    )
    return jax.shard_map(
        per_device,
        mesh=mesh,
        in_specs=placed,
        out_specs=(
            P("dp", "tensor"),
            P("dp", "tensor"),
            P("tensor", None, "dp", None),
            P(("tensor", "dp"), None),
            P("dp", "tensor"),
        ),
        check_vma=False,
    )
```

```python
import functools

import jax
import jax.numpy as jnp
from jax import lax
from jax.experimental import pallas as pl
from jax.experimental.pallas import tpu as pltpu
from jax.sharding import PartitionSpec as P

BLK = 256
LOG = 4


ROOT_HALF = 0.7071067811865476
INV_ROOT_TWO_PI = 0.3989422804014327
BF16 = jnp.bfloat16
F32 = jnp.float32


def swapped(block, axis, mask):
    count = lax.axis_size(axis)
    return lax.ppermute(block, axis, [(i, i ^ mask) for i in range(count)])


def summed_over(part, axis):
    count = lax.axis_size(axis)
    total = part.astype(F32)
    for mask in range(1, count):
        total = total + swapped(part, axis, mask).astype(F32)
    return total.astype(BF16)


def gelu_pair(preact):
    cdf = 0.5 * (1.0 + lax.erf(preact * ROOT_HALF))
    return (preact * cdf, cdf + preact * INV_ROOT_TWO_PI * jnp.exp(-0.5 * preact * preact))


def nt_dot(a, b):
    return lax.dot_general(a, b, (((1,), (1,)), ((), ())), preferred_element_type=F32)


def core_swap(x):
    return swapped(x, "dp", 1)


def moved(x, shift, sources):
    pairs = [(2 * p + c, 2 * (p + shift) + c) for p in sources for c in range(2)]
    return lax.ppermute(x, "dp", pairs)


def line_gather(x):
    chips = lax.axis_size("dp") // 2
    chip = lax.axis_index("dp") // 2
    from_left, from_right = [x], [x]
    for step in range(1, chips):
        from_left.append(moved(from_left[-1], 1, range(step - 1, chips - 1)))
        from_right.append(moved(from_right[-1], -1, range(1, chips - step + 1)))
    slots = [x] + [
        jnp.where(chip >= j, from_left[j], from_right[chips - j]) for j in range(1, chips)
    ]
    own = jnp.stack(slots)
    return own, core_swap(own)


def rows_gather(x):
    chips = lax.axis_size("dp") // 2
    if chips > 4:
        return lax.all_gather(x, "dp", axis=0, tiled=True)
    chip, core = lax.axis_index("dp") // 2, lax.axis_index("dp") % 2
    own, other = line_gather(x)
    first = core == 0
    both = jnp.stack([jnp.where(first, own, other), jnp.where(first, other, own)], axis=1)
    slots = [
        lax.dynamic_index_in_dim(both, (chip - s + chips) % chips, 0, keepdims=False)
        for s in range(chips)
    ]
    return jnp.stack(slots).reshape((2 * chips * x.shape[0],) + x.shape[1:])


def rows_scatter(x):
    chips = lax.axis_size("dp") // 2
    if chips > 4:
        return lax.psum_scatter(x, "dp", scatter_dimension=0, tiled=True)
    by_owner = x.reshape((chips, 2, -1) + x.shape[1:])
    core = lax.axis_index("dp") % 2
    mine = lax.dynamic_index_in_dim(by_owner, core, 1, keepdims=False)
    theirs = lax.dynamic_index_in_dim(by_owner, 1 - core, 1, keepdims=False)
    return line_scatter(mine, theirs)


def line_scatter(mine, theirs):
    chips = lax.axis_size("dp") // 2
    chip = lax.axis_index("dp") // 2
    pair = (mine.astype(F32) + core_swap(theirs).astype(F32)).astype(BF16)
    pick = lambda index: lax.dynamic_index_in_dim(
        pair, jnp.clip(index, 0, chips - 1), 0, keepdims=False
    ).astype(F32)
    right = left = None
    for step in range(1, chips):
        going_right, going_left = pick(chip + chips - step), pick(chip - chips + step)
        if right is not None:
            going_right = going_right + right.astype(F32)
            going_left = going_left + left.astype(F32)
        right = moved(going_right.astype(BF16), 1, range(0, step))
        left = moved(going_left.astype(BF16), -1, range(chips - step, chips))
    return (pick(chip) + right.astype(F32) + left.astype(F32)).astype(BF16)


def chunk_kernel(factors, local, aliased, *refs):
    pieces = refs[:factors]
    cot_ref, w_ref, right_ref = refs[factors:factors + 3]
    rest = refs[factors + 3 + aliased:]
    hidden_ref, dw_ref, dright_ref, loc_ref = rest[:4]
    far_refs = rest[4:4 + factors - 1 - local]
    low_ref = rest[4 + factors - 1 - local]
    depth = (factors - 1) * BLK
    x, xt, acc = rest[-3:]
    step = pl.program_id(0)

    @pl.when(step == 0)
    def _():
        for k in range(factors):
            piece = pieces[k][...]
            x[:, k * BLK:(k + 1) * BLK] = piece
            xt[k * BLK:(k + 1) * BLK, :] = piece.T

    w, right = w_ref[0], right_ref[...]
    preact = jnp.dot(x[:, :depth], w, preferred_element_type=F32)
    preact = preact + jnp.dot(x[:, depth:], right, preferred_element_type=F32)
    act, slope = gelu_pair(preact)
    hidden_ref[...] = act.astype(BF16)
    grad = (cot_ref[...].astype(F32) * slope).astype(BF16)
    dw_ref[0] = jnp.dot(xt[:depth, :], grad, preferred_element_type=F32).astype(BF16)
    dright_ref[...] = jnp.dot(xt[depth:, :], grad, preferred_element_type=F32).astype(BF16)
    back, low_back = nt_dot(grad, w), nt_dot(grad, right)

    @pl.when(step == 0)
    def _():
        acc[:, :depth] = back
        acc[:, depth:] = low_back

    @pl.when(step > 0)
    def _():
        acc[:, :depth] += back
        acc[:, depth:] += low_back

    @pl.when(step == pl.num_programs(0) - 1)
    def _():
        loc_ref[...] = acc[:, :local * BLK]
        for i, far in enumerate(far_refs):
            far[...] = acc[:, (local + i) * BLK:(local + i + 1) * BLK].astype(BF16)
        low_ref[...] = acc[:, (factors - 1) * BLK:]


def run_chunk(q, at, ratio, local, piece_arrays, piece_cols, cot, w, right, previous):
    rows, wide = cot.shape
    factors = len(piece_arrays)
    depth = factors * BLK
    n_far = factors - 1 - local
    column = lambda col: pl.BlockSpec((rows, BLK), lambda h: (0, col))
    in_specs = [column(col) for col in piece_cols]
    in_specs += [
        pl.BlockSpec((rows, BLK), lambda h: (0, q * ratio + h)),
        pl.BlockSpec((1, depth - BLK, BLK), lambda h: (at * ratio + h, 0, 0)),
        pl.BlockSpec((BLK, BLK), lambda h: (0, q * ratio + h)),
    ]
    args = list(piece_arrays) + [cot, w, right]
    aliases = {}
    for output, array in enumerate(previous):
        if array is not None:
            aliases[len(args)] = output
            args.append(array)
            in_specs.append(pl.BlockSpec(memory_space=pl.ANY))
    whole = lambda cols: pl.BlockSpec((rows, cols), lambda h: (0, 0))
    out_specs = [
        pl.BlockSpec((rows, BLK), lambda h: (0, q * ratio + h)),
        pl.BlockSpec((1, depth - BLK, BLK), lambda h: (at * ratio + h, 0, 0)),
        pl.BlockSpec((BLK, BLK), lambda h: (0, q * ratio + h)),
        whole(local * BLK),
    ] + [whole(BLK)] * (n_far + 1)
    out_shape = [
        jax.ShapeDtypeStruct((rows, wide), BF16),
        jax.ShapeDtypeStruct(w.shape, BF16),
        jax.ShapeDtypeStruct(right.shape, BF16),
        jax.ShapeDtypeStruct((rows, local * BLK), F32),
    ] + [jax.ShapeDtypeStruct((rows, BLK), BF16)] * n_far + [jax.ShapeDtypeStruct((rows, BLK), F32)]
    return pl.pallas_call(
        functools.partial(chunk_kernel, factors, local, len(aliases)),
        grid=(ratio,),
        in_specs=in_specs,
        out_specs=out_specs,
        out_shape=out_shape,
        scratch_shapes=[
            pltpu.VMEM((rows, depth), BF16),
            pltpu.VMEM((depth, rows), BF16),
            pltpu.VMEM((rows, depth), F32),
        ],
        input_output_aliases=aliases,
        cost_estimate=pl.CostEstimate(
            flops=6 * rows * depth * BLK * ratio,
            bytes_accessed=2 * (2 * ratio * depth * BLK + 2 * rows * ratio * BLK + 5 * rows * depth // 2),
            transcendentals=2 * rows * ratio * BLK,
        ),
        compiler_params=pltpu.CompilerParams(
            dimension_semantics=("arbitrary",), vmem_limit_bytes=40 * 1024 * 1024
        ),
    )(*args)


def final_kernel(blocks, local_masks, n_far, *refs):
    locs = refs[:blocks]
    fars = refs[blocks:blocks + n_far * blocks]
    grad_low, left, out = refs[blocks + n_far * blocks:]
    for j in range(blocks):
        total = nt_dot(grad_low[...], left[j * BLK:(j + 1) * BLK, :])
        for k, mask in enumerate(local_masks):
            total = total + locs[j ^ mask][:, k * BLK:(k + 1) * BLK]
        for i in range(n_far):
            total = total + fars[i * blocks + j][...].astype(F32)
        out[:, j * BLK:(j + 1) * BLK] = total.astype(BF16)


def per_device(tokens, butterfly, left_factor, right_factor, cotangent):
    rows = tokens.shape[0]
    blocks = tokens.shape[1] // BLK
    hidden_blocks = right_factor.shape[1] // BLK
    ratio = hidden_blocks // blocks
    local_masks = [0] + [1 << b for b in range(LOG) if 1 << b < blocks]
    far_masks = [(1 << b) // blocks for b in range(LOG) if 1 << b >= blocks]
    n_far = len(far_masks)
    factors = LOG + 2

    weights = []
    span = max(1, blocks // 2)
    for first in range(0, blocks, span):
        part = slice(first * ratio, (first + span) * ratio)
        full = lax.all_gather(butterfly[part], "dp", axis=2, tiled=True)
        weights.append(full.reshape(span * ratio, (factors - 1) * BLK, BLK))

    left_full = lax.all_gather(left_factor, "dp", axis=0, tiled=True)
    far_tokens = [swapped(tokens, "tensor", mask) for mask in far_masks]
    low_part = jnp.dot(tokens, left_full, preferred_element_type=F32).astype(BF16)
    low = summed_over(low_part, "tensor")
    right_own, _ = lax.optimization_barrier((right_factor, low_part))
    right_full = rows_gather(right_own)

    hidden = dw = dright = None
    locs, fars, low_back, grads = [], [[] for _ in far_masks], None, []
    for q in range(blocks):
        at = q % span
        arrays = [tokens] * len(local_masks) + far_tokens + [low]
        columns = [q ^ mask for mask in local_masks] + [q] * n_far + [0]
        hidden, dw, dright, loc, *more = run_chunk(
            q, at, ratio, len(local_masks), arrays, columns, cotangent, weights[q // span],
            right_full, (hidden, dw if at else None, dright),
        )
        if at == span - 1:
            blocks_dw = dw.reshape(span * ratio, factors - 1, BLK, BLK)
            grads.append(lax.psum_scatter(blocks_dw, "dp", scatter_dimension=2, tiled=True))
        locs.append(loc)
        for i, mask in enumerate(far_masks):
            fars[i].append(swapped(more[i], "tensor", mask))
        low_back = more[-1] if low_back is None else low_back + more[-1]

    grad_low = summed_over(low_back.astype(BF16), "tensor")
    grad_first = jnp.einsum("td,tr->dr", tokens, grad_low, preferred_element_type=F32)
    sum_first = rows_scatter(grad_first.astype(BF16))
    sum_second = rows_scatter(dright)
    grad_tokens = pl.pallas_call(
        functools.partial(final_kernel, blocks, local_masks, n_far),
        out_shape=jax.ShapeDtypeStruct(tokens.shape, BF16),
        in_specs=[pl.BlockSpec(memory_space=pltpu.VMEM)] * (blocks + n_far * blocks + 2),
        out_specs=pl.BlockSpec(memory_space=pltpu.VMEM),
        cost_estimate=pl.CostEstimate(
            flops=2 * rows * blocks * BLK * BLK,
            bytes_accessed=rows * blocks * BLK * (4 * len(local_masks) + 2 * n_far + 2),
            transcendentals=0,
        ),
        compiler_params=pltpu.CompilerParams(vmem_limit_bytes=40 * 1024 * 1024),
    )(*locs, *[f for level in fars for f in level], grad_low, left_full)

    sum_weight = jnp.concatenate(grads, axis=0)
    return (hidden, grad_tokens, sum_weight, sum_first, sum_second)


def solution(mesh):
    placed = (
        P("dp", "tensor"),
        P("tensor", None, "dp", None),
        P(("tensor", "dp"), None),
        P("dp", "tensor"),
        P("dp", "tensor"),
    )
    return jax.shard_map(
        per_device,
        mesh=mesh,
        in_specs=placed,
        out_specs=(
            P("dp", "tensor"),
            P("dp", "tensor"),
            P("tensor", None, "dp", None),
            P(("tensor", "dp"), None),
            P("dp", "tensor"),
        ),
        check_vma=False,
    )
```
